32 devices in a mesh: row: 2 (over core), col: 4 (over y, x), ch: 4 (over z).
Axes of the slice: x: 2, y: 2, z: 4, core: 2. Of those that a mesh axis runs over, the one named last changes fastest.
Arguments:
- grad_out: float32 [4096, 1024], P(('row', 'col'), 'ch'), may hold values from -6 to 6
- relu_mask: int32 [4096, 1024], P(('row', 'col'), 'ch'), may hold values 0 or 1
- saved_agg: float32 [4096, 1024], P(('row', 'col'), 'ch'), may hold values from -0.1875 to 0.1875
- weight: float32 [1024, 1024], P('ch'), may hold values from -0.1875 to 0.1875
- tile_vals: float32 [2, 4, 128, 128, 128], P('row', 'col'), may hold values from -0.125 to 0.125
- tile_pos: int32 [2, 4, 128], P('row', 'col'), may hold values from 0 to 127, as said below
- tile_count: int32 [2, 4], P('row', 'col'), may hold values from 32 to 128, as said below
Outputs:
- weight_grad: float32 [1024, 1024], P(('row', 'col'), 'ch')
- input_grad: float32 [4096, 1024], P('col', 'ch')
The draws below stay inside these ranges and needn't reach their ends.
Inputs may be any that keep to these rules, and one draw needn't show every extreme that they name: `tile_pos`: each block's entries are a permutation of 0 to 127; the first tile_count of them are the block's nonzero tiles, the others list its zero tiles and their slots' values are ignored. `tile_count`: some block is full in every draw.
All inputs are finite; a program needn't handle non-finite values. No bound on the sum of `relu_mask` on one device may be relied on, other than what follows from the above.
Results may differ from the reference program's by a relative error of at most 0.0003.
Values sent between devices are 32-bit elements; how exact they have to be, the bound alone decides.
A program may use at most 128 MiB of HBM per device.

```python
import jax
import jax.numpy as jnp
from jax import lax

F = 1024
TILE = 128
OUT_TILES = 16
IN_TILES = 8
BLOCK_TILES = 128
ROWS_OUT = 4096
ROWS_IN = 4096
N_ROW = 2
N_COL = 4


def draw_tile_pos(key, part):
    row_groups = ROWS_OUT // (TILE * OUT_TILES)
    col_groups = ROWS_IN // (TILE * IN_TILES)
    block_keys = jax.random.split(jax.random.fold_in(key, 11), row_groups * col_groups)
    orders = jax.vmap(lambda single: jax.random.permutation(single, BLOCK_TILES))(block_keys)
    return orders.reshape(row_groups, col_groups, BLOCK_TILES).astype(jnp.int32)


def draw_tile_count(key, part):
    row_groups = ROWS_OUT // (TILE * OUT_TILES)
    col_groups = ROWS_IN // (TILE * IN_TILES)
    lowest = max(BLOCK_TILES // 4, 1)
    counts = jax.random.randint(jax.random.fold_in(key, 23), (row_groups * col_groups,), lowest, BLOCK_TILES + 1)
    chosen = jax.random.randint(jax.random.fold_in(key, 29), (), 0, row_groups * col_groups)
    counts = jnp.where(jnp.arange(row_groups * col_groups, dtype=jnp.int32) == chosen, BLOCK_TILES, counts)
    return counts.reshape(row_groups, col_groups).astype(jnp.int32)


def touch_ends(array, stream_key, least, top_value):
    spot = [jax.random.randint(jax.random.fold_in(stream_key, axis), (), 0, length) for axis, length in enumerate(array.shape)]
    main_axis = array.shape.index(max(array.shape))
    next_to = spot[:main_axis] + [(spot[main_axis] + 1) % array.shape[main_axis]] + spot[main_axis + 1:]
    return array.at[tuple(spot)].set(least).at[tuple(next_to)].set(top_value)


def strengthened(drawn, key, source, target, blocks, factor):
    def block_of(dim):
        return (jnp.arange(drawn.shape[dim]) // (drawn.shape[dim] // blocks)).reshape((-1,) + (1,) * (drawn.ndim - 1 - dim))

    one_side = jax.random.permutation(key, blocks)[block_of(target)]
    other_side = (block_of(target) + blocks // 2) % blocks
    return jnp.where((block_of(source) == one_side) | (block_of(source) == other_side), factor * drawn, drawn)


def block_scale(rng, extent, cuts, least, largest):
    def one(axis_at, parts):
        draws = jax.random.uniform(jax.random.fold_in(jax.random.fold_in(rng, 6), axis_at), (parts,), jnp.float32, least / len(cuts), largest / len(cuts))
        return jnp.repeat(jnp.exp(draws), extent[axis_at] // parts).reshape((-1,) + (1,) * (len(extent) - axis_at - 1))

    factor_of = one(*cuts[0])
    for cut in cuts[1:]:
        factor_of = factor_of * one(*cut)
    return factor_of


def noise(own_key, shape, spread, limit, shards=(), held_as=jnp.bfloat16):
    factor_of = block_scale(own_key, shape, shards, -0.22, 0.18) if shards else 1.0
    drawn = jax.random.normal(own_key, shape, jnp.float32) * spread * factor_of
    return jnp.minimum(jnp.maximum(drawn, -limit), limit).astype(held_as)


def noise_with(rng, shape, width, bound, cuts, heavy, kind=jnp.bfloat16):
    result = width * jax.random.normal(rng, shape, jnp.float32)
    if cuts:
        result = result * block_scale(rng, shape, cuts, -0.22, 0.18)
    return jnp.clip(strengthened(result, jax.random.fold_in(rng, 3), *heavy), -bound, bound).astype(kind)


def setup_inputs(seed: int = 0) -> dict:
    splits = jax.random.split(jax.random.key(seed), 8)
    grad_out = noise(splits[0], (ROWS_OUT, F), 1.0, 6.0, ((0, 8), (1, 4)), jnp.float32)
    relu_mask = touch_ends((jax.random.randint(splits[1], (ROWS_OUT, F), 0, 2) < 1).astype(jnp.int32), jax.random.fold_in(splits[1], 1), 0, 1)
    saved_agg = noise_with(splits[2], (ROWS_OUT, F), (2.0 / ROWS_OUT ** 0.5), 0.1875, ((0, 8), (1, 4)), (0, 1, 8, 2.0), jnp.float32)
    weight = noise(splits[3], (F, F), F ** -0.5, 0.1875, ((0, 4),), jnp.float32)
    tile_vals = noise(splits[4], (N_ROW, N_COL, BLOCK_TILES, TILE, TILE), (TILE * OUT_TILES * N_ROW // 2) ** -0.5, 0.125, ((0, 2), (1, 4)), jnp.float32)
    tile_pos = draw_tile_pos(jax.random.fold_in(splits[7], 71), 0)
    tile_count = draw_tile_count(jax.random.fold_in(splits[7], 71), 0)
    return dict(grad_out=grad_out, relu_mask=relu_mask, saved_agg=saved_agg, weight=weight, tile_vals=tile_vals, tile_pos=tile_pos, tile_count=tile_count)


HIGHEST = lax.Precision.HIGHEST

def block_grad(tile_set, positions, live_count, grad_rows):
    slot_total = tile_set.shape[0]
    channels = grad_rows.shape[1]
    active = (jnp.arange(slot_total, dtype=jnp.int32) < live_count).astype(jnp.float32)
    out_tile = (positions // IN_TILES).astype(jnp.int32)
    in_tile = (positions % IN_TILES).astype(jnp.int32)
    blocks = grad_rows.reshape(OUT_TILES, TILE, channels)
    picked = jnp.take(blocks, out_tile, axis=0)
    product = jnp.einsum('tij,tif->tjf', tile_set, picked, precision=HIGHEST)
    onehot = (in_tile[:, None] == jnp.arange(IN_TILES, dtype=jnp.int32)[None, :]).astype(jnp.float32) * active[:, None]
    summed = jnp.einsum('tc,tjf->cjf', onehot, product, precision=HIGHEST)
    return summed.reshape(IN_TILES * TILE, channels)

def reference(grad_out, relu_mask, saved_agg, weight, tile_vals, tile_pos, tile_count):
    masked = grad_out * relu_mask.astype(jnp.float32)
    weight_grad = jnp.dot(saved_agg.T, masked, precision=HIGHEST, preferred_element_type=jnp.float32)
    agg_grad = jnp.dot(masked, weight.T, precision=HIGHEST, preferred_element_type=jnp.float32)
    row_groups = tile_vals.shape[0]
    col_groups = tile_vals.shape[1]
    channels = agg_grad.shape[1]
    grad_blocks = agg_grad.reshape(row_groups, OUT_TILES * TILE, channels)

    def per_column(col_index):

        def add_block(running, row_index):
            return (running + block_grad(tile_vals[row_index, col_index], tile_pos[row_index, col_index], tile_count[row_index, col_index], grad_blocks[row_index]), None)
        running, _ = lax.scan(add_block, jnp.zeros((IN_TILES * TILE, channels), jnp.float32), jnp.arange(row_groups, dtype=jnp.int32))
        return running
    input_grad = lax.map(per_column, jnp.arange(col_groups, dtype=jnp.int32))
    return (weight_grad, input_grad.reshape(col_groups * IN_TILES * TILE, channels))
```

```python
import functools

import jax
import jax.numpy as jnp
from jax import lax
from jax.experimental import pallas as pl
from jax.experimental.pallas import tpu as pltpu
from jax.sharding import PartitionSpec as P

TILE = 128
MESH = pl.DeviceIdType.MESH
F32 = jnp.float32
BF16 = jnp.bfloat16


def split(x):
    hi = x.astype(BF16)
    return hi, (x - hi.astype(F32)).astype(BF16)


def nn(a, b):
    return lax.dot_general(a, b, (((1,), (0,)), ((), ())), preferred_element_type=F32)


def nt(a, b):
    return lax.dot_general(a, b, (((1,), (1,)), ((), ())), preferred_element_type=F32)


def kernel(
    R, C, N, K,
    slot_ref, g_ref, mask_ref, sa_hbm, w_hbm, tiles_hbm,
    wg_ref, ig_ref,
    M, G, tiles, at_hi, at_lo, w_f, w_hi, w_lo, sa, g_hi, g_lo, acc,
    wgp, wgr, wgs, wgc, wgo, igr,
    local_sem, zsend, zrecv, csend, crecv, wrsend, wrrecv, wcsend, wcrecv, wfsend, wfrecv,
    irsend, irrecv, iasend, iarecv,
):
    r, c, z = lax.axis_index("row"), lax.axis_index("col"), lax.axis_index("ch")
    HB, D = M.shape[2], M.shape[3]
    RC = R * C
    per = RC // N
    blk = wgp.shape[1]
    slots = tiles.shape[0]
    IN = acc.shape[0]
    in_tiles = IN // TILE
    tpb = HB // TILE
    piece = IN // R

    cp_w = pltpu.make_async_copy(w_hbm, w_f, local_sem.at[0])
    cp_sa = pltpu.make_async_copy(sa_hbm, sa, local_sem.at[1])
    cp_t = pltpu.make_async_copy(tiles_hbm, tiles, local_sem.at[2])
    cp_w.start()
    cp_sa.start()
    cp_t.start()

    def dev(r_, c_, z_):
        return {"row": r_, "col": c_, "ch": z_}

    q = r * C + c
    d_idx = z * per + q // N
    d_r, d_c, d_z = d_idx // C, d_idx % C, q % N
    s_q = (q % per) * N + z
    s_r, s_c, s_z = s_q // C, s_q % C, q // per
    away = jnp.logical_not((d_r == r) & (d_c == c) & (d_z == z))

    barrier = pltpu.get_barrier_semaphore()

    def hello(r_, c_, z_):
        pl.semaphore_signal(barrier, inc=1, device_id=dev(r_, c_, z_), device_id_type=MESH)

    for j in range(1, R):
        hello((r + j) % R, c, z)
    for j in range(1, C):
        hello(r, (c + j) % C, z)

    @pl.when(z > 0)
    def _():
        hello(r, c, z - 1)

    @pl.when(z < N - 1)
    def _():
        hello(r, c, z + 1)

    @pl.when(away)
    def _():
        hello(d_r, d_c, d_z)
        hello(s_r, s_c, s_z)

    def own(k):
        rows = pl.ds(pl.multiple_of(k * HB, HB), HB)
        M[z, k] = g_ref[rows, :] * mask_ref[rows, :].astype(F32)

    own(0)
    own(1)
    one_if = lambda cond: jnp.where(cond, 1, 0)
    greeted = R - 1 + C - 1 + one_if(z > 0) + one_if(z < N - 1) + 2 * one_if(away)
    pl.semaphore_wait(barrier, greeted)

    def zcopy(origin, k, step):
        way = 0 if step < 0 else 1
        return pltpu.make_async_remote_copy(
            src_ref=M.at[origin, k], dst_ref=M.at[origin, k],
            send_sem=zsend.at[way, origin, k], recv_sem=zrecv.at[origin, k],
            device_id=dev(r, c, z + step), device_id_type=MESH,
        )

    def own_send(k):
        @pl.when(z > 0)
        def _():
            zcopy(z, k, -1).start()

        @pl.when(z < N - 1)
        def _():
            zcopy(z, k, 1).start()

    own_send(0)
    own_send(1)
    acc[...] = jnp.zeros_like(acc)
    wgp[...] = jnp.zeros_like(wgp)
    cp_w.wait()
    for n in range(N):
        cols = slice(n * D, (n + 1) * D)
        w_hi[:, cols], w_lo[:, cols] = split(w_f[:, cols])
    cp_sa.wait()
    cp_t.wait()

    def prep(k, cc):
        for t in range(tpb):
            def one(i, _):
                p = ((cc * K + k) * tpb + t) * in_tiles + i
                v = slot_ref[p]
                tile = tiles[lax.rem(v, slots)]
                tile = jnp.where(v < slots, tile, jnp.zeros_like(tile))
                hi, lo = split(tile.T)
                rows = pl.ds(pl.multiple_of(i * TILE, TILE), TILE)
                cols = slice(cc * HB + t * TILE, cc * HB + (t + 1) * TILE)
                at_hi[k, rows, cols] = hi
                at_lo[k, rows, cols] = lo
                return 0

            lax.fori_loop(0, in_tiles, one, 0, unroll=2)

    def ccopy(k, j):
        return pltpu.make_async_remote_copy(
            src_ref=G.at[k, c], dst_ref=G.at[k, c],
            send_sem=csend.at[k, j], recv_sem=crecv.at[k, j],
            device_id=dev(r, (c + j) % C, z), device_id_type=MESH,
        )

    def cwait(k, j):
        o = (c + C - j) % C
        return pltpu.make_async_remote_copy(
            src_ref=G.at[k, o], dst_ref=G.at[k, o],
            send_sem=csend.at[k, j], recv_sem=crecv.at[k, j],
            device_id=dev(r, (c + j) % C, z), device_id_type=MESH,
        )

    def consume(k):
        for j in range(1, C):
            cwait(k, j).wait_recv()
        for n in range(C):
            rows = slice(n * HB, (n + 1) * HB)
            g_hi[rows, :], g_lo[rows, :] = split(G[k, n])

        def part(i, _):
            rows = pl.ds(pl.multiple_of(i * 256, 256), 256)
            a = at_hi[k, rows, :]
            acc[rows, :] += nn(a, g_hi[...]) + nn(a, g_lo[...]) + nn(at_lo[k, rows, :], g_hi[...])
            return 0

        lax.fori_loop(0, IN // 256, part, 0)

    groups = [[] for _ in range(N - 1)]
    for cc in range(C):
        groups[cc * (N - 1) // C].append(cc)

    def body(k, _):
        for d in range(1, N):
            for cc in groups[d - 1]:
                prep(k, cc)

            @pl.when(z >= d)
            def _():
                zcopy(z - d, k, 1).wait_recv()

                @pl.when(z < N - 1)
                def _():
                    zcopy(z - d, k, 1).start()

            @pl.when(z + d < N)
            def _():
                zcopy(z + d, k, -1).wait_recv()

                @pl.when(z > 0)
                def _():
                    zcopy(z + d, k, -1).start()

            if d == 1:
                @pl.when(k + 2 < K)
                def _():
                    own(k + 2)
                    own_send(k + 2)

        agg = jnp.zeros((HB, D), F32)
        for n in range(N):
            cols = slice(n * D, (n + 1) * D)
            hi, lo = split(M[n, k])
            agg += nt(hi, w_hi[:, cols]) + nt(lo, w_hi[:, cols]) + nt(hi, w_lo[:, cols])
        G[k, c] = agg
        for j in range(1, C):
            ccopy(k, j).start()

        rows = pl.ds(pl.multiple_of(k * HB, HB), HB)
        s_hi, s_lo = split(sa[rows, :].T)
        for n in range(N):
            hi, lo = split(M[n, k])
            res = nn(s_hi, hi) + nn(s_hi, lo) + nn(s_lo, hi)
            for h in range(per):
                wgp[h * N + n] += res[h * blk:(h + 1) * blk, :]

        @pl.when(k > 0)
        def _():
            consume(k - 1)

        return 0

    lax.fori_loop(0, K, body, 0)

    def wrcopy(j):
        t = (r + j) % R
        return pltpu.make_async_remote_copy(
            src_ref=wgp.at[pl.ds(t * C, C)], dst_ref=wgr.at[j],
            send_sem=wrsend.at[j], recv_sem=wrrecv.at[j],
            device_id=dev(t, c, z), device_id_type=MESH,
        )

    def wccopy(j):
        t = (c + j) % C
        return pltpu.make_async_remote_copy(
            src_ref=wgs.at[t], dst_ref=wgc.at[j],
            send_sem=wcsend.at[j], recv_sem=wcrecv.at[j],
            device_id=dev(r, t, z), device_id_type=MESH,
        )

    wfcopy = pltpu.make_async_remote_copy(
        src_ref=wgo, dst_ref=wg_ref, send_sem=wfsend, recv_sem=wfrecv,
        device_id=dev(d_r, d_c, d_z), device_id_type=MESH,
    )

    def ircopy(j):
        t = (r + j) % R
        return pltpu.make_async_remote_copy(
            src_ref=acc.at[pl.ds(pl.multiple_of(t * piece, piece), piece)], dst_ref=igr.at[j],
            send_sem=irsend.at[j], recv_sem=irrecv.at[j],
            device_id=dev(t, c, z), device_id_type=MESH,
        )

    mine = pl.ds(pl.multiple_of(r * piece, piece), piece)

    def iacopy(j):
        return pltpu.make_async_remote_copy(
            src_ref=ig_ref.at[mine], dst_ref=ig_ref.at[mine],
            send_sem=iasend.at[j], recv_sem=iarecv.at[j],
            device_id=dev((r + j) % R, c, z), device_id_type=MESH,
        )

    def iawait(j):
        theirs = pl.ds(pl.multiple_of(((r + R - j) % R) * piece, piece), piece)
        return pltpu.make_async_remote_copy(
            src_ref=ig_ref.at[theirs], dst_ref=ig_ref.at[theirs],
            send_sem=iasend.at[j], recv_sem=iarecv.at[j],
            device_id=dev((r + j) % R, c, z), device_id_type=MESH,
        )

    for j in range(1, R):
        wrcopy(j).start()
    for j in range(1, R):
        wrcopy(j).wait_recv()
    total = wgp[pl.ds(r * C, C)]
    for j in range(1, R):
        total += wgr[j]
    wgs[...] = total
    for j in range(1, C):
        wccopy(j).start()

    consume(K - 1)
    for j in range(1, R):
        ircopy(j).start()
    for j in range(1, R):
        ircopy(j).wait_recv()
    summed = acc[mine, :]
    for j in range(1, R):
        summed += igr[j]
    ig_ref[mine, :] = summed
    for j in range(1, R):
        iacopy(j).start()

    for j in range(1, C):
        wccopy(j).wait_recv()
    wpart = wgs[c]
    for j in range(1, C):
        wpart += wgc[j]

    @pl.when(away)
    def _():
        wgo[...] = wpart
        wfcopy.start()
        wfcopy.wait()

    @pl.when(jnp.logical_not(away))
    def _():
        wg_ref[...] = wpart

    for j in range(1, R):
        iawait(j).wait_recv()

    for j in range(1, R):
        wrcopy(j).wait_send()
        ircopy(j).wait_send()
        iacopy(j).wait_send()
    for j in range(1, C):
        wccopy(j).wait_send()

    def drain(k, _):
        for j in range(1, C):
            ccopy(k, j).wait_send()
        for n in range(N):
            @pl.when((z > 0) & (z <= n))
            def _():
                zcopy(n, k, -1).wait_send()

            @pl.when((z < N - 1) & (z >= n))
            def _():
                zcopy(n, k, 1).wait_send()

        return 0

    lax.fori_loop(0, K, drain, 0)


def per_device(R, C, N, grad_out, relu_mask, saved_agg, weight, tile_vals, tile_pos, tile_count):
    H, D = grad_out.shape
    F = weight.shape[1]
    tiles = tile_vals[0, 0]
    slots = tiles.shape[0]
    out_rows = C * H
    IN = slots * TILE * TILE // out_rows
    HB = TILE
    K = H // HB
    blk = F // (R * C)
    s = jnp.arange(slots, dtype=jnp.int32)
    code = jnp.where(s < tile_count[0, 0], s, s + slots)
    where = jnp.sum(jnp.where(tile_pos[0, 0][None, :] == s[:, None], code[None, :], 0), axis=1).astype(jnp.int32)
    vmem = pl.BlockSpec(memory_space=pltpu.VMEM)
    hbm = pl.BlockSpec(memory_space=pl.ANY)
    dma = pltpu.SemaphoreType.DMA
    return pl.pallas_call(
        functools.partial(kernel, R, C, N, K),
        out_shape=(
            jax.ShapeDtypeStruct((blk, D), F32),
            jax.ShapeDtypeStruct((IN, D), F32),
        ),
        in_specs=[pl.BlockSpec(memory_space=pltpu.SMEM), vmem, vmem, hbm, hbm, hbm],
        out_specs=(vmem, vmem),
        scratch_shapes=[
            pltpu.VMEM((N, K, HB, D), F32),
            pltpu.VMEM((K, C, HB, D), F32),
            pltpu.VMEM((slots, TILE, TILE), F32),
            pltpu.VMEM((K, IN, C * HB), BF16),
            pltpu.VMEM((K, IN, C * HB), BF16),
            pltpu.VMEM((D, F), F32),
            pltpu.VMEM((D, F), BF16),
            pltpu.VMEM((D, F), BF16),
            pltpu.VMEM((H, D), F32),
            pltpu.VMEM((C * HB, D), BF16),
            pltpu.VMEM((C * HB, D), BF16),
            pltpu.VMEM((IN, D), F32),
            pltpu.VMEM((R * C, blk, D), F32),
            pltpu.VMEM((R, C, blk, D), F32),
            pltpu.VMEM((C, blk, D), F32),
            pltpu.VMEM((C, blk, D), F32),
            pltpu.VMEM((blk, D), F32),
            pltpu.VMEM((R, IN // R, D), F32),
            dma((3,)),
            dma((2, N, K)), dma((N, K)),
            dma((K, C)), dma((K, C)),
            dma((R,)), dma((R,)),
            dma((C,)), dma((C,)),
            dma, dma,
            dma((R,)), dma((R,)),
            dma((R,)), dma((R,)),
        ],
        compiler_params=pltpu.CompilerParams(
            collective_id=0, has_side_effects=True, vmem_limit_bytes=60 * 1024 * 1024
        ),
    )(where, grad_out, relu_mask, saved_agg, weight, tiles)


def solution(mesh):
    in_specs = (
        P(("row", "col"), "ch"),
        P(("row", "col"), "ch"),
        P(("row", "col"), "ch"),
        P("ch", None),
        P("row", "col", None, None, None),
        P("row", "col", None),
        P("row", "col"),
    )
    out_specs = (P(("row", "col"), "ch"), P("col", "ch"))
    R, C, N = mesh.shape["row"], mesh.shape["col"], mesh.shape["ch"]
    return jax.shard_map(
        functools.partial(per_device, R, C, N), mesh=mesh, in_specs=in_specs, out_specs=out_specs, check_vma=False
    )
```

```python
import functools

import jax
import jax.numpy as jnp
from jax import lax
from jax.experimental import pallas as pl
from jax.experimental.pallas import tpu as pltpu
from jax.sharding import PartitionSpec as P

TILE = 128
MESH = pl.DeviceIdType.MESH
F32 = jnp.float32
BF16 = jnp.bfloat16


def split(x):
    hi = x.astype(BF16)
    return hi, (x - hi.astype(F32)).astype(BF16)


def nn(a, b):
    return lax.dot_general(a, b, (((1,), (0,)), ((), ())), preferred_element_type=F32)


def nt(a, b):
    return lax.dot_general(a, b, (((1,), (1,)), ((), ())), preferred_element_type=F32)


def kernel(
    R, C, N, K,
    slot_ref, g_ref, mask_ref, sa_hbm, w_hbm, tiles_hbm,
    wg_ref, ig_ref, igr,
    M, G, tiles, at_hi, at_lo, w_f, w_hi, w_lo, sa, sa_far, g_hi, g_lo,
    wgp, wgr, wgs, wgc, wgo,
    local_sem, zsend, zrecv, csend, crecv, wrsend, wrrecv, wcsend, wcrecv, wfsend, wfrecv,
    irsend, irrecv, iasend, iarecv, sasend, sarecv,
):
    r, c, z = lax.axis_index("row"), lax.axis_index("col"), lax.axis_index("ch")
    HB, D = M.shape[2], M.shape[3]
    RC = R * C
    per = RC // N
    blk = wgp.shape[2]
    slots = tiles.shape[0]
    acc = ig_ref
    IN = acc.shape[0]
    in_tiles = IN // TILE
    tpb = HB // TILE
    piece = IN // R

    cp_w = pltpu.make_async_copy(w_hbm, w_f, local_sem.at[0])
    cp_sa = pltpu.make_async_copy(sa_hbm, sa, local_sem.at[1])
    cp_t = pltpu.make_async_copy(tiles_hbm, tiles, local_sem.at[2])
    cp_w.start()
    cp_sa.start()
    cp_t.start()

    def dev(r_, c_, z_):
        return {"row": r_, "col": c_, "ch": z_}

    q = r * C + c
    mid = (z > 0) & (z < N - 1)
    hosts = (z == 1) | (z == N - 2)
    far = jnp.where(z == 1, 0, N - 1)
    step_in = jnp.where(z == 0, 1, -1)

    def dest(zi):
        idx = zi * per + q // N
        return idx // C, idx % C, q % N

    def is_me(o):
        return (o[0] == r) & (o[1] == c) & (o[2] == z)

    dests = (dest(z), dest(far))
    active = (mid, hosts)
    away = tuple(a & jnp.logical_not(is_me(o)) for a, o in zip(active, dests))
    home = tuple(a & is_me(o) for a, o in zip(active, dests))
    s_q = (q % per) * N + z
    s_z = jnp.minimum(jnp.maximum(q // per, 1), N - 2)
    source = (s_q // C, s_q % C, s_z)
    fed = jnp.logical_not(is_me(source))

    barrier = pltpu.get_barrier_semaphore()

    def hello(r_, c_, z_):
        pl.semaphore_signal(barrier, inc=1, device_id=dev(r_, c_, z_), device_id_type=MESH)

    for j in range(1, R):
        hello((r + j) % R, c, z)
    for j in range(1, C):
        hello(r, (c + j) % C, z)

    @pl.when(z > 0)
    def _():
        hello(r, c, z - 1)

    @pl.when(z < N - 1)
    def _():
        hello(r, c, z + 1)

    for s in range(2):
        @pl.when(away[s])
        def _():
            hello(*dests[s])

    @pl.when(fed)
    def _():
        hello(*source)

    def own(k):
        rows = pl.ds(pl.multiple_of(k * HB, HB), HB)
        M[z, k] = g_ref[rows, :] * mask_ref[rows, :].astype(F32)

    own(0)
    own(1)
    one_if = lambda cond: jnp.where(cond, 1, 0)
    greeted = R - 1 + C - 1 + one_if(z > 0) + one_if(z < N - 1) + one_if(fed) + one_if(away[0]) + one_if(away[1])
    pl.semaphore_wait(barrier, greeted)

    def zcopy(origin, k, step):
        way = 0 if step < 0 else 1
        return pltpu.make_async_remote_copy(
            src_ref=M.at[origin, k], dst_ref=M.at[origin, k],
            send_sem=zsend.at[way, origin, k], recv_sem=zrecv.at[origin, k],
            device_id=dev(r, c, z + step), device_id_type=MESH,
        )

    def sacopy(k, step):
        rows = pl.ds(pl.multiple_of(k * HB, HB), HB)
        return pltpu.make_async_remote_copy(
            src_ref=sa.at[rows], dst_ref=sa_far.at[rows],
            send_sem=sasend.at[k], recv_sem=sarecv.at[k],
            device_id=dev(r, c, z + step), device_id_type=MESH,
        )

    def own_send(k):
        @pl.when(z > 0)
        def _():
            zcopy(z, k, -1).start()

        @pl.when(z < N - 1)
        def _():
            zcopy(z, k, 1).start()

        @pl.when(jnp.logical_not(mid))
        def _():
            sacopy(k, step_in).start()

    cp_sa.wait()
    own_send(0)
    own_send(1)
    acc[...] = jnp.zeros_like(acc)
    wgp[...] = jnp.zeros_like(wgp)
    cp_w.wait()
    for n in range(N):
        cols = slice(n * D, (n + 1) * D)
        w_hi[:, cols], w_lo[:, cols] = split(w_f[:, cols])
    cp_t.wait()

    def prep(k, cc):
        for t in range(tpb):
            def one(i, _):
                p = ((cc * K + k) * tpb + t) * in_tiles + i
                v = slot_ref[p]
                tile = tiles[lax.rem(v, slots)]
                tile = jnp.where(v < slots, tile, jnp.zeros_like(tile))
                hi, lo = split(tile.T)
                rows = pl.ds(pl.multiple_of(i * TILE, TILE), TILE)
                cols = slice(cc * HB + t * TILE, cc * HB + (t + 1) * TILE)
                at_hi[k, rows, cols] = hi
                at_lo[k, rows, cols] = lo
                return 0

            lax.fori_loop(0, in_tiles, one, 0, unroll=2)

    def ccopy(k, j):
        return pltpu.make_async_remote_copy(
            src_ref=G.at[k, c], dst_ref=G.at[k, c],
            send_sem=csend.at[k, j], recv_sem=crecv.at[k, j],
            device_id=dev(r, (c + j) % C, z), device_id_type=MESH,
        )

    def cwait(k, j):
        o = (c + C - j) % C
        return pltpu.make_async_remote_copy(
            src_ref=G.at[k, o], dst_ref=G.at[k, o],
            send_sem=csend.at[k, j], recv_sem=crecv.at[k, j],
            device_id=dev(r, (c + j) % C, z), device_id_type=MESH,
        )

    def consume(k):
        for j in range(1, C):
            cwait(k, j).wait_recv()
        for n in range(C):
            rows = slice(n * HB, (n + 1) * HB)
            g_hi[rows, :], g_lo[rows, :] = split(G[k, n])

        def part(i, _):
            rows = pl.ds(pl.multiple_of(i * 256, 256), 256)
            a = at_hi[k, rows, :]
            acc[rows, :] += nn(a, g_hi[...]) + nn(a, g_lo[...]) + nn(at_lo[k, rows, :], g_hi[...])
            return 0

        lax.fori_loop(0, IN // 256, part, 0)

    def wrcopy(s, j):
        t = (r + j) % R
        return pltpu.make_async_remote_copy(
            src_ref=wgp.at[s, pl.ds(t * C, C)], dst_ref=wgr.at[s, j],
            send_sem=wrsend.at[s, j], recv_sem=wrrecv.at[s, j],
            device_id=dev(t, c, z), device_id_type=MESH,
        )

    def wccopy(s, j):
        t = (c + j) % C
        return pltpu.make_async_remote_copy(
            src_ref=wgs.at[s, t], dst_ref=wgc.at[s, j],
            send_sem=wcsend.at[s, j], recv_sem=wcrecv.at[s, j],
            device_id=dev(r, t, z), device_id_type=MESH,
        )

    def wfcopy(s):
        return pltpu.make_async_remote_copy(
            src_ref=wgo.at[s], dst_ref=wg_ref, send_sem=wfsend.at[s], recv_sem=wfrecv,
            device_id=dev(*dests[s]), device_id_type=MESH,
        )

    groups = [[] for _ in range(N - 1)]
    for cc in range(C):
        groups[cc * (N - 1) // C].append(cc)

    def body(k, _):
        for d in range(1, N):
            for cc in groups[d - 1]:
                prep(k, cc)

            @pl.when(z >= d)
            def _():
                zcopy(z - d, k, 1).wait_recv()

                @pl.when(z < N - 1)
                def _():
                    zcopy(z - d, k, 1).start()

            @pl.when(z + d < N)
            def _():
                zcopy(z + d, k, -1).wait_recv()

                @pl.when(z > 0)
                def _():
                    zcopy(z + d, k, -1).start()

            if d == 1:
                @pl.when(k + 2 < K)
                def _():
                    own(k + 2)
                    own_send(k + 2)

        agg = jnp.zeros((HB, D), F32)
        for n in range(N):
            cols = slice(n * D, (n + 1) * D)
            hi, lo = split(M[n, k])
            agg += nt(hi, w_hi[:, cols]) + nt(lo, w_hi[:, cols]) + nt(hi, w_lo[:, cols])
        G[k, c] = agg
        for j in range(1, C):
            ccopy(k, j).start()

        rows = pl.ds(pl.multiple_of(k * HB, HB), HB)

        def grad(s, ref):
            s_hi, s_lo = split(ref[rows, :].T)
            for n in range(N):
                hi, lo = split(M[n, k])
                res = nn(s_hi, hi) + nn(s_hi, lo) + nn(s_lo, hi)
                for h in range(per):
                    wgp[s, h * N + n] += res[h * blk:(h + 1) * blk, :]

        @pl.when(mid)
        def _():
            grad(0, sa)

        @pl.when(hosts)
        def _():
            sacopy(k, step_in).wait_recv()
            grad(1, sa_far)

        @pl.when(k == K - 1)
        def _():
            for s in range(2):
                @pl.when(active[s])
                def _():
                    for j in range(1, R):
                        wrcopy(s, j).start()

        @pl.when(k > 0)
        def _():
            consume(k - 1)

        return 0

    lax.fori_loop(0, K, body, 0)

    def ircopy(j):
        t = (r + j) % R
        whole = R == 2
        rows = pl.ds(0, IN) if whole else pl.ds(pl.multiple_of(t * piece, piece), piece)
        return pltpu.make_async_remote_copy(
            src_ref=acc.at[rows], dst_ref=igr if whole else igr.at[j],
            send_sem=irsend.at[j], recv_sem=irrecv.at[j],
            device_id=dev(t, c, z), device_id_type=MESH,
        )

    mine = pl.ds(pl.multiple_of(r * piece, piece), piece)

    def iacopy(j):
        return pltpu.make_async_remote_copy(
            src_ref=ig_ref.at[mine], dst_ref=ig_ref.at[mine],
            send_sem=iasend.at[j], recv_sem=iarecv.at[j],
            device_id=dev((r + j) % R, c, z), device_id_type=MESH,
        )

    def iawait(j):
        theirs = pl.ds(pl.multiple_of(((r + R - j) % R) * piece, piece), piece)
        return pltpu.make_async_remote_copy(
            src_ref=ig_ref.at[theirs], dst_ref=ig_ref.at[theirs],
            send_sem=iasend.at[j], recv_sem=iarecv.at[j],
            device_id=dev((r + j) % R, c, z), device_id_type=MESH,
        )

    def fold_rows(s):
        for j in range(1, R):
            wrcopy(s, j).wait_recv()
        total = wgp[s, pl.ds(r * C, C)]
        for j in range(1, R):
            total += wgr[s, j]
        wgs[s] = total
        for j in range(1, C):
            wccopy(s, j).start()

    def fold_cols(s):
        for j in range(1, C):
            wccopy(s, j).wait_recv()
        total = wgs[s, c]
        for j in range(1, C):
            total += wgc[s, j]

        @pl.when(away[s])
        def _():
            wgo[s] = total
            wfcopy(s).start()

        @pl.when(home[s])
        def _():
            wg_ref[...] = total

    for s in range(2):
        pl.when(active[s])(functools.partial(fold_rows, s))
    consume(K - 1)
    for j in range(1, R):
        ircopy(j).start()
    for s in range(2):
        pl.when(active[s])(functools.partial(fold_cols, s))
    for j in range(1, R):
        ircopy(j).wait_recv()
    if R > 2:
        summed = acc[mine, :]
        for j in range(1, R):
            summed += igr[j]
        ig_ref[mine, :] = summed
        for j in range(1, R):
            iacopy(j).start()
        for j in range(1, R):
            iawait(j).wait_recv()

    @pl.when(fed)
    def _():
        wfcopy(0).wait_recv()

    for s in range(2):
        @pl.when(active[s])
        def _():
            for j in range(1, R):
                wrcopy(s, j).wait_send()
            for j in range(1, C):
                wccopy(s, j).wait_send()

        @pl.when(away[s])
        def _():
            wfcopy(s).wait_send()

    for j in range(1, R):
        ircopy(j).wait_send()
        if R > 2:
            iacopy(j).wait_send()

    def drain(k, _):
        @pl.when(jnp.logical_not(mid))
        def _():
            sacopy(k, step_in).wait_send()

        for j in range(1, C):
            ccopy(k, j).wait_send()
        for n in range(N):
            @pl.when((z > 0) & (z <= n))
            def _():
                zcopy(n, k, -1).wait_send()

            @pl.when((z < N - 1) & (z >= n))
            def _():
                zcopy(n, k, 1).wait_send()

        return 0

    lax.fori_loop(0, K, drain, 0)


def per_device(R, C, N, grad_out, relu_mask, saved_agg, weight, tile_vals, tile_pos, tile_count):
    H, D = grad_out.shape
    F = weight.shape[1]
    tiles = tile_vals[0, 0]
    slots = tiles.shape[0]
    out_rows = C * H
    IN = slots * TILE * TILE // out_rows
    HB = TILE
    K = H // HB
    blk = F // (R * C)
    s = jnp.arange(slots, dtype=jnp.int32)
    code = jnp.where(s < tile_count[0, 0], s, s + slots)
    where = jnp.sum(jnp.where(tile_pos[0, 0][None, :] == s[:, None], code[None, :], 0), axis=1).astype(jnp.int32)
    vmem = pl.BlockSpec(memory_space=pltpu.VMEM)
    hbm = pl.BlockSpec(memory_space=pl.ANY)
    dma = pltpu.SemaphoreType.DMA
    assert N >= 4
    igr_shape = (IN, D) if R == 2 else (R, IN // R, D)
    wg, ig, igr = pl.pallas_call(
        functools.partial(kernel, R, C, N, K),
        out_shape=(
            jax.ShapeDtypeStruct((blk, D), F32),
            jax.ShapeDtypeStruct((IN, D), F32),
            jax.ShapeDtypeStruct(igr_shape, F32),
        ),
        in_specs=[pl.BlockSpec(memory_space=pltpu.SMEM), vmem, vmem, hbm, hbm, hbm],
        out_specs=(vmem, vmem, vmem),
        scratch_shapes=[
            pltpu.VMEM((N, K, HB, D), F32),
            pltpu.VMEM((K, C, HB, D), F32),
            pltpu.VMEM((slots, TILE, TILE), F32),
            pltpu.VMEM((K, IN, C * HB), BF16),
            pltpu.VMEM((K, IN, C * HB), BF16),
            pltpu.VMEM((D, F), F32),
            pltpu.VMEM((D, F), BF16),
            pltpu.VMEM((D, F), BF16),
            pltpu.VMEM((H, D), F32),
            pltpu.VMEM((H, D), F32),
            pltpu.VMEM((C * HB, D), BF16),
            pltpu.VMEM((C * HB, D), BF16),
            pltpu.VMEM((2, R * C, blk, D), F32),
            pltpu.VMEM((2, R, C, blk, D), F32),
            pltpu.VMEM((2, C, blk, D), F32),
            pltpu.VMEM((2, C, blk, D), F32),
            pltpu.VMEM((2, blk, D), F32),
            dma((3,)),
            dma((2, N, K)), dma((N, K)),
            dma((K, C)), dma((K, C)),
            dma((2, R)), dma((2, R)),
            dma((2, C)), dma((2, C)),
            dma((2,)), dma,
            dma((R,)), dma((R,)),
            dma((R,)), dma((R,)),
            dma((K,)), dma((K,)),
        ],
        compiler_params=pltpu.CompilerParams(
            collective_id=0, has_side_effects=True, vmem_limit_bytes=60 * 1024 * 1024
        ),
    )(where, grad_out, relu_mask, saved_agg, weight, tiles)

    def finish(wg_in, a, b, wg_out, ig_out):
        wg_out[...] = wg_in[...]
        ig_out[...] = a[...] + b[...] if R == 2 else a[...]

    return pl.pallas_call(
        finish,
        out_shape=(jax.ShapeDtypeStruct((blk, D), F32), jax.ShapeDtypeStruct((IN, D), F32)),
        in_specs=[vmem, vmem, vmem if R == 2 else hbm],
        out_specs=(vmem, vmem),
    )(wg, ig, igr)


def solution(mesh):
    in_specs = (
        P(("row", "col"), "ch"),
        P(("row", "col"), "ch"),
        P(("row", "col"), "ch"),
        P("ch", None),
        P("row", "col", None, None, None),
        P("row", "col", None),
        P("row", "col"),
    )
    out_specs = (P(("row", "col"), "ch"), P("col", "ch"))
    R, C, N = mesh.shape["row"], mesh.shape["col"], mesh.shape["ch"]
    return jax.shard_map(
        functools.partial(per_device, R, C, N), mesh=mesh, in_specs=in_specs, out_specs=out_specs, check_vma=False
    )
```

```python
import functools

import jax
import jax.numpy as jnp
from jax import lax
from jax.experimental import pallas as pl
from jax.experimental.pallas import tpu as pltpu
from jax.sharding import PartitionSpec as P

TILE = 128
MESH = pl.DeviceIdType.MESH
F32 = jnp.float32
BF16 = jnp.bfloat16


def split(x):
    hi = x.astype(BF16)
    return hi, (x - hi.astype(F32)).astype(BF16)


def nn(a, b):
    return lax.dot_general(a, b, (((1,), (0,)), ((), ())), preferred_element_type=F32)


def nt(a, b):
    return lax.dot_general(a, b, (((1,), (1,)), ((), ())), preferred_element_type=F32)


def kernel(
    R, C, N, K,
    slot_ref, g_ref, mask_ref, sa_hbm, w_hbm, tiles_hbm,
    wg_ref, ig_ref, igr,
    M, G, tiles, at_hi, at_lo, w_f, w_hi, w_lo, sa, g_hi, g_lo,
    wgp, wgr, wgs, wgc, wgo,
    local_sem, zsend, zrecv, csend, crecv, wrsend, wrrecv, wcsend, wcrecv, wfsend, wfrecv,
    irsend, irrecv, iasend, iarecv,
):
    r, c, z = lax.axis_index("row"), lax.axis_index("col"), lax.axis_index("ch")
    HB, D = M.shape[2], M.shape[3]
    RC = R * C
    per = RC // N
    blk = wgp.shape[1]
    slots = tiles.shape[0]
    acc = ig_ref
    IN = acc.shape[0]
    in_tiles = IN // TILE
    tpb = HB // TILE
    piece = IN // R

    cp_w = pltpu.make_async_copy(w_hbm, w_f, local_sem.at[0])
    cp_sa = pltpu.make_async_copy(sa_hbm, sa, local_sem.at[1])
    cp_t = pltpu.make_async_copy(tiles_hbm, tiles, local_sem.at[2])
    cp_w.start()
    cp_sa.start()
    cp_t.start()

    def dev(r_, c_, z_):
        return {"row": r_, "col": c_, "ch": z_}

    q = r * C + c
    d_idx = z * per + q // N
    d_r, d_c, d_z = d_idx // C, d_idx % C, q % N
    s_q = (q % per) * N + z
    s_r, s_c, s_z = s_q // C, s_q % C, q // per
    away = jnp.logical_not((d_r == r) & (d_c == c) & (d_z == z))

    barrier = pltpu.get_barrier_semaphore()

    def hello(r_, c_, z_):
        pl.semaphore_signal(barrier, inc=1, device_id=dev(r_, c_, z_), device_id_type=MESH)

    for j in range(1, R):
        hello((r + j) % R, c, z)
    for j in range(1, C):
        hello(r, (c + j) % C, z)

    @pl.when(z > 0)
    def _():
        hello(r, c, z - 1)

    @pl.when(z < N - 1)
    def _():
        hello(r, c, z + 1)

    @pl.when(away)
    def _():
        hello(d_r, d_c, d_z)
        hello(s_r, s_c, s_z)

    def own(k):
        rows = pl.ds(pl.multiple_of(k * HB, HB), HB)
        M[z, k] = g_ref[rows, :] * mask_ref[rows, :].astype(F32)

    own(0)
    own(1)
    one_if = lambda cond: jnp.where(cond, 1, 0)
    greeted = R - 1 + C - 1 + one_if(z > 0) + one_if(z < N - 1) + 2 * one_if(away)
    pl.semaphore_wait(barrier, greeted)

    def zcopy(origin, k, step):
        way = 0 if step < 0 else 1
        return pltpu.make_async_remote_copy(
            src_ref=M.at[origin, k], dst_ref=M.at[origin, k],
            send_sem=zsend.at[way, origin, k], recv_sem=zrecv.at[origin, k],
            device_id=dev(r, c, z + step), device_id_type=MESH,
        )

    def own_send(k):
        @pl.when(z > 0)
        def _():
            zcopy(z, k, -1).start()

        @pl.when(z < N - 1)
        def _():
            zcopy(z, k, 1).start()

    own_send(0)
    own_send(1)
    acc[...] = jnp.zeros_like(acc)
    wgp[...] = jnp.zeros_like(wgp)
    cp_w.wait()
    for n in range(N):
        cols = slice(n * D, (n + 1) * D)
        w_hi[:, cols], w_lo[:, cols] = split(w_f[:, cols])
    cp_sa.wait()
    cp_t.wait()

    def prep(k, cc):
        for t in range(tpb):
            def one(i, _):
                p = ((cc * K + k) * tpb + t) * in_tiles + i
                v = slot_ref[p]
                tile = tiles[lax.rem(v, slots)]
                tile = jnp.where(v < slots, tile, jnp.zeros_like(tile))
                hi, lo = split(tile.T)
                rows = pl.ds(pl.multiple_of(i * TILE, TILE), TILE)
                cols = slice(cc * HB + t * TILE, cc * HB + (t + 1) * TILE)
                at_hi[k, rows, cols] = hi
                at_lo[k, rows, cols] = lo
                return 0

            lax.fori_loop(0, in_tiles, one, 0, unroll=2)

    def ccopy(k, j):
        return pltpu.make_async_remote_copy(
            src_ref=G.at[k, c], dst_ref=G.at[k, c],
            send_sem=csend.at[k, j], recv_sem=crecv.at[k, j],
            device_id=dev(r, (c + j) % C, z), device_id_type=MESH,
        )

    def cwait(k, j):
        o = (c + C - j) % C
        return pltpu.make_async_remote_copy(
            src_ref=G.at[k, o], dst_ref=G.at[k, o],
            send_sem=csend.at[k, j], recv_sem=crecv.at[k, j],
            device_id=dev(r, (c + j) % C, z), device_id_type=MESH,
        )

    def consume(k):
        for j in range(1, C):
            cwait(k, j).wait_recv()
        for n in range(C):
            rows = slice(n * HB, (n + 1) * HB)
            g_hi[rows, :], g_lo[rows, :] = split(G[k, n])

        def part(i, _):
            rows = pl.ds(pl.multiple_of(i * 256, 256), 256)
            a = at_hi[k, rows, :]
            acc[rows, :] += nn(a, g_hi[...]) + nn(a, g_lo[...]) + nn(at_lo[k, rows, :], g_hi[...])
            return 0

        lax.fori_loop(0, IN // 256, part, 0)

    def wrcopy(j):
        t = (r + j) % R
        return pltpu.make_async_remote_copy(
            src_ref=wgp.at[pl.ds(t * C, C)], dst_ref=wgr.at[j],
            send_sem=wrsend.at[j], recv_sem=wrrecv.at[j],
            device_id=dev(t, c, z), device_id_type=MESH,
        )

    groups = [[] for _ in range(N - 1)]
    for cc in range(C):
        groups[cc * max(N - 2, 1) // C].append(cc)

    def body(k, _):
        for d in range(1, N):
            @pl.when(z >= d)
            def _():
                zcopy(z - d, k, 1).wait_recv()

                @pl.when(z < N - 1)
                def _():
                    zcopy(z - d, k, 1).start()

            @pl.when(z + d < N)
            def _():
                zcopy(z + d, k, -1).wait_recv()

                @pl.when(z > 0)
                def _():
                    zcopy(z + d, k, -1).start()

            if d == 1:
                @pl.when(k + 2 < K)
                def _():
                    own(k + 2)
                    own_send(k + 2)

            for cc in groups[d - 1]:
                prep(k, cc)

        agg = jnp.zeros((HB, D), F32)
        for n in range(N):
            cols = slice(n * D, (n + 1) * D)
            hi, lo = split(M[n, k])
            agg += nt(hi, w_hi[:, cols]) + nt(lo, w_hi[:, cols]) + nt(hi, w_lo[:, cols])
        G[k, c] = agg
        for j in range(1, C):
            ccopy(k, j).start()

        rows = pl.ds(pl.multiple_of(k * HB, HB), HB)
        s_hi, s_lo = split(sa[rows, :].T)
        for n in range(N):
            hi, lo = split(M[n, k])
            res = nn(s_hi, hi) + nn(s_hi, lo) + nn(s_lo, hi)
            for h in range(per):
                wgp[h * N + n] += res[h * blk:(h + 1) * blk, :]

        @pl.when(k == K - 1)
        def _():
            for j in range(1, R):
                wrcopy(j).start()

        @pl.when(k > 0)
        def _():
            consume(k - 1)

        return 0

    lax.fori_loop(0, K, body, 0)

    def wccopy(j):
        t = (c + j) % C
        return pltpu.make_async_remote_copy(
            src_ref=wgs.at[t], dst_ref=wgc.at[j],
            send_sem=wcsend.at[j], recv_sem=wcrecv.at[j],
            device_id=dev(r, t, z), device_id_type=MESH,
        )

    wfcopy = pltpu.make_async_remote_copy(
        src_ref=wgo, dst_ref=wg_ref, send_sem=wfsend, recv_sem=wfrecv,
        device_id=dev(d_r, d_c, d_z), device_id_type=MESH,
    )

    def ircopy(j):
        t = (r + j) % R
        whole = R == 2
        rows = pl.ds(0, IN) if whole else pl.ds(pl.multiple_of(t * piece, piece), piece)
        return pltpu.make_async_remote_copy(
            src_ref=acc.at[rows], dst_ref=igr if whole else igr.at[j],
            send_sem=irsend.at[j], recv_sem=irrecv.at[j],
            device_id=dev(t, c, z), device_id_type=MESH,
        )

    mine = pl.ds(pl.multiple_of(r * piece, piece), piece)

    def iacopy(j):
        return pltpu.make_async_remote_copy(
            src_ref=ig_ref.at[mine], dst_ref=ig_ref.at[mine],
            send_sem=iasend.at[j], recv_sem=iarecv.at[j],
            device_id=dev((r + j) % R, c, z), device_id_type=MESH,
        )

    def iawait(j):
        theirs = pl.ds(pl.multiple_of(((r + R - j) % R) * piece, piece), piece)
        return pltpu.make_async_remote_copy(
            src_ref=ig_ref.at[theirs], dst_ref=ig_ref.at[theirs],
            send_sem=iasend.at[j], recv_sem=iarecv.at[j],
            device_id=dev((r + j) % R, c, z), device_id_type=MESH,
        )

    for j in range(1, R):
        wrcopy(j).wait_recv()
    total = wgp[pl.ds(r * C, C)]
    for j in range(1, R):
        total += wgr[j]
    wgs[...] = total
    for j in range(1, C):
        wccopy(j).start()

    consume(K - 1)
    for j in range(1, R):
        ircopy(j).start()
    for j in range(1, C):
        wccopy(j).wait_recv()
    wpart = wgs[c]
    for j in range(1, C):
        wpart += wgc[j]

    @pl.when(away)
    def _():
        wgo[...] = wpart
        wfcopy.start()
        wfcopy.wait()

    @pl.when(jnp.logical_not(away))
    def _():
        wg_ref[...] = wpart

    for j in range(1, R):
        ircopy(j).wait_recv()
    if R > 2:
        summed = acc[mine, :]
        for j in range(1, R):
            summed += igr[j]
        ig_ref[mine, :] = summed
        for j in range(1, R):
            iacopy(j).start()
        for j in range(1, R):
            iawait(j).wait_recv()

    for j in range(1, R):
        wrcopy(j).wait_send()
        ircopy(j).wait_send()
        if R > 2:
            iacopy(j).wait_send()
    for j in range(1, C):
        wccopy(j).wait_send()

    def drain(k, _):
        for j in range(1, C):
            ccopy(k, j).wait_send()
        for n in range(N):
            @pl.when((z > 0) & (z <= n))
            def _():
                zcopy(n, k, -1).wait_send()

            @pl.when((z < N - 1) & (z >= n))
            def _():
                zcopy(n, k, 1).wait_send()

        return 0

    lax.fori_loop(0, K, drain, 0)


def per_device(R, C, N, grad_out, relu_mask, saved_agg, weight, tile_vals, tile_pos, tile_count):
    H, D = grad_out.shape
    F = weight.shape[1]
    tiles = tile_vals[0, 0]
    slots = tiles.shape[0]
    out_rows = C * H
    IN = slots * TILE * TILE // out_rows
    HB = TILE
    K = H // HB
    blk = F // (R * C)
    s = jnp.arange(slots, dtype=jnp.int32)
    code = jnp.where(s < tile_count[0, 0], s, s + slots)
    where = jnp.sum(jnp.where(tile_pos[0, 0][None, :] == s[:, None], code[None, :], 0), axis=1).astype(jnp.int32)
    vmem = pl.BlockSpec(memory_space=pltpu.VMEM)
    hbm = pl.BlockSpec(memory_space=pl.ANY)
    dma = pltpu.SemaphoreType.DMA
    igr_shape = (IN, D) if R == 2 else (R, IN // R, D)
    wg, ig, igr = pl.pallas_call(
        functools.partial(kernel, R, C, N, K),
        out_shape=(
            jax.ShapeDtypeStruct((blk, D), F32),
            jax.ShapeDtypeStruct((IN, D), F32),
            jax.ShapeDtypeStruct(igr_shape, F32),
        ),
        in_specs=[pl.BlockSpec(memory_space=pltpu.SMEM), vmem, vmem, hbm, hbm, hbm],
        out_specs=(vmem, vmem, vmem),
        scratch_shapes=[
            pltpu.VMEM((N, K, HB, D), F32),
            pltpu.VMEM((K, C, HB, D), F32),
            pltpu.VMEM((slots, TILE, TILE), F32),
            pltpu.VMEM((K, IN, C * HB), BF16),
            pltpu.VMEM((K, IN, C * HB), BF16),
            pltpu.VMEM((D, F), F32),
            pltpu.VMEM((D, F), BF16),
            pltpu.VMEM((D, F), BF16),
            pltpu.VMEM((H, D), F32),
            pltpu.VMEM((C * HB, D), BF16),
            pltpu.VMEM((C * HB, D), BF16),
            pltpu.VMEM((R * C, blk, D), F32),
            pltpu.VMEM((R, C, blk, D), F32),
            pltpu.VMEM((C, blk, D), F32),
            pltpu.VMEM((C, blk, D), F32),
            pltpu.VMEM((blk, D), F32),
            dma((3,)),
            dma((2, N, K)), dma((N, K)),
            dma((K, C)), dma((K, C)),
            dma((R,)), dma((R,)),
            dma((C,)), dma((C,)),
            dma, dma,
            dma((R,)), dma((R,)),
            dma((R,)), dma((R,)),
        ],
        compiler_params=pltpu.CompilerParams(
            collective_id=0, has_side_effects=True, vmem_limit_bytes=60 * 1024 * 1024
        ),
    )(where, grad_out, relu_mask, saved_agg, weight, tiles)

    def finish(wg_in, a, b, wg_out, ig_out):
        wg_out[...] = wg_in[...]
        ig_out[...] = a[...] + b[...] if R == 2 else a[...]

    return pl.pallas_call(
        finish,
        out_shape=(jax.ShapeDtypeStruct((blk, D), F32), jax.ShapeDtypeStruct((IN, D), F32)),
        in_specs=[vmem, vmem, vmem if R == 2 else hbm],
        out_specs=(vmem, vmem),
    )(wg, ig, igr)


def solution(mesh):
    in_specs = (
        P(("row", "col"), "ch"),
        P(("row", "col"), "ch"),
        P(("row", "col"), "ch"),
        P("ch", None),
        P("row", "col", None, None, None),
        P("row", "col", None),
        P("row", "col"),
    )
    out_specs = (P(("row", "col"), "ch"), P("col", "ch"))
    R, C, N = mesh.shape["row"], mesh.shape["col"], mesh.shape["ch"]
    return jax.shard_map(
        functools.partial(per_device, R, C, N), mesh=mesh, in_specs=in_specs, out_specs=out_specs, check_vma=False
    )
```
